32 devices in a mesh: groups: 2 (over y), tok: 8 (over z, x), head: 2 (over core).
Axes of the slice: x: 2, y: 2, z: 4, core: 2. Of those that a mesh axis runs over, the one named last changes fastest.
Arguments:
- interior_element_embedding: bfloat16 [2048, 1024], P(('groups', 'tok')), parts along dimension 0, may hold values from -70 to 70
- boundary_element_embedding: bfloat16 [512, 1024], P(('groups', 'tok')), parts along dimension 0, may hold values from -70 to 70
- interior_landmark_position: int32 [256], P(('groups', 'tok')), parts along dimension 0, may hold values from 0 to 1023, as said below
- boundary_landmark_position: int32 [128], P(('groups', 'tok')), parts along dimension 0, may hold values from 0 to 255, as said below
- interior_rescaling_factor: float32 [1024], replicated, may hold values from 0.1 to 1.9
- boundary_rescaling_factor: float32 [1024], replicated, may hold values from 0.1 to 1.9
- question_projection_matrix: bfloat16 [1024, 1024], P(None, 'head'), may hold values from -0.1875 to 0.1875
- lookup_projection_matrix: bfloat16 [1024, 1024], P(None, 'head'), may hold values from -0.1875 to 0.1875
- content_projection_matrix: bfloat16 [1024, 1024], P(None, 'head'), may hold values from -0.1875 to 0.1875
- final_projection_matrix: bfloat16 [1024, 1024], P('head'), may hold values from -0.1875 to 0.1875
- channel_logit_divisor: float32 [16], P('head'), may hold values from 0.5 to 96
Outputs:
- update: bfloat16 [2048, 1024], P(('groups', 'tok'), 'head'), parts along dimension 0
The draws below stay inside these ranges and needn't reach their ends.
There are 2 independent parts, one for each index of `groups`. The reference program is written for one: setup_inputs(seed, part) draws one part's arguments, and reference() takes and returns one part's arrays. A program takes and returns all parts, laid end to end along the dimension named above; an argument that names none is the same for every part. Nothing has to cross between parts.
Inputs may be any that keep to these rules, and one draw needn't show every extreme that they name: `interior_landmark_position`: anchor i lies among the 128 cells of block i // 16, that is from (i // 16) * 128 on; no cell is named twice; cell 0 and the last cell of the last block are always anchors. `boundary_landmark_position`: anchor i lies among the 32 cells of block i // 8, that is from (i // 8) * 32 on; no cell is named twice; cell 0 and the last cell of the last block are always anchors.
All inputs are finite; a program needn't handle non-finite values.
Results may differ from the reference program's by a relative error of at most 0.012.
The reference program's roundings to bfloat16 on the way (of `vol_normed`, `surf_normed`, `anchors`, `queries`, `anchor_keys`, `anchor_values`, `rounded` and `context`) count: a program that leaves them out, or rounds other values in their place, can miss the bound.
Values may be sent and summed in bfloat16 or wider, within the bound.
A program may use at most 64 MiB of HBM per device.

```python
import math
import jax
import jax.numpy as jnp
from jax import lax

D = 1024
HEADS = 16
CV_DEV = 128
VA_DEV = 16
SA_DEV = 8
CS_DEV = 32
VCELLS = 1024
SCELLS = 256
VA = 128
SA = 64


def scaled_cells(key, row_count):
    subkeys = jax.random.split(key, 3)
    entries = jnp.clip(jax.random.normal(subkeys[0], (row_count, D), jnp.float32), -4.0, 4.0)
    row_scale = jnp.exp(jax.random.uniform(subkeys[2], (row_count, 1), jnp.float32, 0.0, math.log(10.0)))
    column_scale = jnp.exp(jax.random.uniform(subkeys[1], (1, D), jnp.float32, 0.0, math.log(10.0)))
    return (entries * row_scale * column_scale * 0.1).astype(jnp.bfloat16)


def pick_cells(key, block_count, per_block, picks):
    block_keys = jax.random.split(key, block_count)

    def one_block(block_key, block_number):
        drawn_pick = jax.random.permutation(block_key, per_block)[:picks].astype(jnp.int32)
        narrow = jax.random.permutation(block_key, per_block - 1)[:picks].astype(jnp.int32)
        first_block = jnp.concatenate([jnp.zeros((1,), jnp.int32), narrow[1:] + 1])
        last_block = jnp.concatenate([jnp.full((1,), per_block - 1, jnp.int32), narrow[1:]])
        chosen = jnp.where(block_number == 0, first_block, jnp.where(block_number == block_count - 1, last_block, drawn_pick))
        return chosen + block_number * per_block
    return jax.vmap(one_block)(block_keys, jnp.arange(block_count, dtype=jnp.int32)).reshape(-1)


def draw_interior_element_embedding(key, part):
    return scaled_cells(jax.random.fold_in(key, 11), VCELLS)


def draw_boundary_element_embedding(key, part):
    return scaled_cells(jax.random.fold_in(key, 12), SCELLS)


def draw_interior_landmark_position(key, part):
    return pick_cells(jax.random.fold_in(key, 21), VA // VA_DEV, CV_DEV, VA_DEV)


def draw_boundary_landmark_position(key, part):
    return pick_cells(jax.random.fold_in(key, 22), SA // SA_DEV, CS_DEV, SA_DEV)


def draw_channel_logit_divisor(key, part):
    subkeys = jax.random.split(jax.random.fold_in(key, 31), 1)
    return jnp.exp(jax.random.uniform(subkeys[0], (HEADS,), jnp.float32, math.log(0.5), math.log(2.0)))


def shard_levels(rng, extent, shards, least, high):
    factor_of, own = 1.0, jax.random.fold_in(rng, 6)
    for position, blocks in shards:
        heights = jnp.exp(jax.random.uniform(jax.random.fold_in(own, position), (blocks,), jnp.float32, least / len(shards), high / len(shards)))
        factor_of = factor_of * jnp.repeat(heights, extent[position] // blocks).reshape([-1 if axis == position else 1 for axis in range(len(extent))])
    return factor_of


def noise(key, shape, width, limit, shards=(), kind=jnp.bfloat16):
    values = width * jax.random.normal(key, shape, jnp.float32)
    if shards:
        values = values * shard_levels(key, shape, shards, -0.22, 0.18)
    return jnp.clip(values, -limit, limit).astype(kind)


def setup_inputs(seed: int = 0, part: int = 0) -> dict:
    key_of = jax.random.split(jax.random.key(seed), 12)
    part_splits = jax.random.split(jax.random.fold_in(key_of[11], part), 12)
    interior_element_embedding = draw_interior_element_embedding(jax.random.fold_in(jax.random.fold_in(key_of[11], part), 71), part)
    boundary_element_embedding = draw_boundary_element_embedding(jax.random.fold_in(jax.random.fold_in(key_of[11], part), 71), part)
    interior_landmark_position = draw_interior_landmark_position(jax.random.fold_in(jax.random.fold_in(key_of[11], part), 71), part)
    boundary_landmark_position = draw_boundary_landmark_position(jax.random.fold_in(jax.random.fold_in(key_of[11], part), 71), part)
    interior_rescaling_factor = jnp.clip(1.0 + 0.18 * jax.random.normal(key_of[4], (D,), jnp.float32), 0.1, 1.9)
    boundary_rescaling_factor = jnp.clip(1.0 + 0.18 * jax.random.normal(key_of[5], (D,), jnp.float32), 0.1, 1.9)
    question_projection_matrix = noise(key_of[6], (D, D), D ** -0.5, 0.1875, ((1, 2),))
    lookup_projection_matrix = noise(key_of[7], (D, D), D ** -0.5, 0.1875, ((1, 2),))
    content_projection_matrix = noise(key_of[8], (D, D), D ** -0.5, 0.1875, ((1, 2),))
    final_projection_matrix = noise(key_of[9], (D, D), D ** -0.5, 0.1875, ((0, 2),))
    channel_logit_divisor = draw_channel_logit_divisor(jax.random.fold_in(key_of[11], 71), part)
    return {"interior_element_embedding": interior_element_embedding, "boundary_element_embedding": boundary_element_embedding, "interior_landmark_position": interior_landmark_position, "boundary_landmark_position": boundary_landmark_position, "interior_rescaling_factor": interior_rescaling_factor, "boundary_rescaling_factor": boundary_rescaling_factor, "question_projection_matrix": question_projection_matrix, "lookup_projection_matrix": lookup_projection_matrix, "content_projection_matrix": content_projection_matrix, "final_projection_matrix": final_projection_matrix, "channel_logit_divisor": channel_logit_divisor}


epsilon = 1e-06

def rms_rows(cells, gain):
    values = cells.astype(jnp.float32)
    mean_square = lax.optimization_barrier(jnp.mean(values * values, axis=1, keepdims=True))
    return (values * lax.rsqrt(mean_square + epsilon) * gain).astype(jnp.bfloat16)

def reference(interior_element_embedding, boundary_element_embedding, interior_landmark_position, boundary_landmark_position, interior_rescaling_factor, boundary_rescaling_factor, question_projection_matrix, lookup_projection_matrix, content_projection_matrix, final_projection_matrix, channel_logit_divisor):
    vol_normed = rms_rows(interior_element_embedding, interior_rescaling_factor)
    surf_normed = rms_rows(jnp.take(boundary_element_embedding, boundary_landmark_position.astype(jnp.int32), axis=0), boundary_rescaling_factor)
    anchors = jnp.concatenate([jnp.take(vol_normed, interior_landmark_position.astype(jnp.int32), axis=0), surf_normed], axis=0)
    queries = jnp.dot(vol_normed, question_projection_matrix, preferred_element_type=jnp.float32).astype(jnp.bfloat16)
    anchor_keys = jnp.dot(anchors, lookup_projection_matrix, preferred_element_type=jnp.float32).astype(jnp.bfloat16)
    anchor_values = jnp.dot(anchors, content_projection_matrix, preferred_element_type=jnp.float32).astype(jnp.bfloat16)
    channel_dimension = D // HEADS
    key_heads = anchor_keys.astype(jnp.float32).reshape(-1, HEADS, channel_dimension)
    value_heads = anchor_values.astype(jnp.float32).reshape(-1, HEADS, channel_dimension)
    logit_multiplier = channel_logit_divisor * (1.0 / math.sqrt(channel_dimension))
    block_rows = math.gcd(VCELLS, 512)
    query_blocks = queries.reshape(VCELLS // block_rows, block_rows, HEADS, channel_dimension)

    def attend(query_block):
        scores = jnp.einsum('qhd,khd->hqk', query_block.astype(jnp.float32), key_heads) * logit_multiplier[:, None, None]
        row_max = lax.optimization_barrier(jnp.max(scores, axis=2, keepdims=True))
        exp_scores = jnp.exp(scores - row_max)
        denominator = lax.optimization_barrier(jnp.sum(exp_scores, axis=2))
        rounded = lax.optimization_barrier(exp_scores.astype(jnp.bfloat16)).astype(jnp.float32)
        accumulated = jnp.einsum('hqk,khd->qhd', rounded, value_heads)
        context = accumulated / jnp.transpose(denominator)[:, :, None]
        return context.reshape(query_block.shape[0], D).astype(jnp.bfloat16)
    context = lax.map(attend, query_blocks).reshape(VCELLS, D)
    mixed_rows = jnp.dot(context, final_projection_matrix, preferred_element_type=jnp.float32)
    mean_square = lax.optimization_barrier(jnp.mean(mixed_rows * mixed_rows, axis=1, keepdims=True))
    return (mixed_rows * lax.rsqrt(mean_square + epsilon)).astype(jnp.bfloat16)
```

```python
import functools
import math

import jax
import jax.numpy as jnp
from jax import lax
from jax.experimental import pallas as pl
from jax.experimental.pallas import tpu as pltpu
from jax.sharding import PartitionSpec as P

epsilon = 1e-06
f32 = jnp.float32
bf16 = jnp.bfloat16


def repeat(count, step):
    if count <= 8:
        for number in range(count):
            step(number)
    else:
        pl.loop(0, count)(step)


def normed(values, gain):
    mean_square = jnp.mean(values * values, axis=1, keepdims=True)
    return (values * lax.rsqrt(mean_square + epsilon) * gain).astype(bf16)


def picked(positions, rows):
    lines = lax.broadcasted_iota(jnp.int32, (rows.shape[0], positions.shape[1]), 0)
    chosen = jnp.where(lines == positions, 1.0, 0.0).astype(bf16)
    return lax.dot_general(
        chosen, rows, (((0,), (0,)), ((), ())), preferred_element_type=f32
    )


def kernel(
    sizes,
    x_hbm,
    surf_hbm,
    vol_pos_hbm,
    surf_pos_hbm,
    vol_gain_hbm,
    surf_gain_hbm,
    wq_hbm,
    wk_hbm,
    wv_hbm,
    wo_hbm,
    scale_hbm,
    out_ref,
    x,
    surf,
    vol_pos,
    surf_pos,
    vol_gain,
    surf_gain,
    wq,
    wk,
    wv,
    wo,
    scale,
    gathered,
    keys,
    values,
    context,
    load_sem,
    major_send,
    minor_send,
    mate_send,
    net_recv,
    mate_recv,
    wo_send,
    wo_recv,
    ctx_send,
    ctx_recv,
):
    tok_count, minor = sizes
    major = tok_count // minor
    me = lax.axis_index("tok")
    core = lax.axis_index("head")
    mate = 1 - core
    row = me // minor
    column = me % minor
    width = x.shape[1]
    half = width // 2
    cells = x.shape[0]
    local_width = wq.shape[1]
    heads = scale.shape[1]
    head_dim = local_width // heads
    pair_width = 2 * head_dim
    pairs = heads // 2

    sources = (
        (x_hbm, x),
        (vol_pos_hbm, vol_pos),
        (surf_hbm, surf),
        (surf_pos_hbm, surf_pos),
        (vol_gain_hbm, vol_gain),
        (surf_gain_hbm, surf_gain),
        (wq_hbm, wq),
        (wk_hbm, wk),
        (wv_hbm, wv),
        (scale_hbm, scale),
    )
    loads = [
        pltpu.make_async_copy(source, target, load_sem.at[number])
        for number, (source, target) in enumerate(sources)
    ]
    for part in range(2):
        loads.append(
            pltpu.make_async_copy(
                wo_hbm.at[:, pl.ds(part * half, half)],
                wo.at[0, part],
                load_sem.at[len(sources) + part],
            )
        )
    for load in loads:
        load.start()

    side = (2 * row) // major

    def far_first(number):
        step = (major - 1 - number) * (1 - side) + (number + 1) * side
        return ((row + step) % major) * minor + column

    def near_first(number):
        step = (number + 1) * (1 - side) + (major - 1 - number) * side
        return ((row + step) % major) * minor + column

    def across(number):
        return row * minor + (column + 1 + number) % minor

    barrier = pltpu.get_barrier_semaphore()
    pl.semaphore_signal(barrier, inc=1, device_id={"head": mate})
    repeat(
        minor - 1,
        lambda number: pl.semaphore_signal(barrier, inc=1, device_id={"tok": across(number)}),
    )
    repeat(
        major - 1,
        lambda number: pl.semaphore_signal(barrier, inc=1, device_id={"tok": far_first(number)}),
    )

    for number in range(6):
        loads[number].wait()
    vol_anchor = normed(picked(vol_pos[...] - me * cells, x[...]), vol_gain[...])
    surf_anchor = normed(picked(surf_pos[...] - me * surf.shape[0], surf[...]), surf_gain[...])
    own = jnp.concatenate([vol_anchor.astype(f32), surf_anchor.astype(f32)], axis=0).astype(bf16)
    gathered[0, me] = own[:, :half]
    gathered[1, me] = own[:, half:]

    pl.semaphore_wait(barrier, major + minor - 1)

    def net_copy(source, send_sem, target):
        return pltpu.make_async_remote_copy(
            src_ref=gathered.at[core, source],
            dst_ref=gathered.at[core, source],
            send_sem=send_sem,
            recv_sem=net_recv.at[source],
            device_id={"tok": target},
        )

    def mate_copy(side_index, source):
        return pltpu.make_async_remote_copy(
            src_ref=gathered.at[side_index, source],
            dst_ref=gathered.at[side_index, source],
            send_sem=mate_send.at[source],
            recv_sem=mate_recv.at[source],
            device_id={"head": mate},
        )

    repeat(
        major - 1,
        lambda number: net_copy(me, major_send.at[number], far_first(number)).start(),
    )
    repeat(
        minor - 1,
        lambda number: net_copy(me, minor_send.at[row], across(number)).start(),
    )
    wo_copies = [
        pltpu.make_async_remote_copy(
            src_ref=wo_hbm.at[:, pl.ds(part * half, half)],
            dst_ref=wo.at[1, part],
            send_sem=wo_send.at[part],
            recv_sem=wo_recv.at[part],
            device_id={"head": mate},
        )
        for part in range(2)
    ]
    for copy in wo_copies:
        copy.start()

    cells_normed = normed(x[...].astype(f32), vol_gain[...])
    loads[6].wait()
    queries = jnp.dot(cells_normed, wq[...], preferred_element_type=f32).astype(bf16)

    def from_across(number):
        source = across(number)
        net_copy(source, minor_send.at[row], source).wait_recv()
        mate_copy(core, source).start()

    repeat(minor - 1, from_across)

    def from_major(number):
        source = near_first(number)
        net_copy(source, minor_send.at[row], source).wait_recv()
        repeat(
            minor - 1,
            lambda step: net_copy(source, minor_send.at[source // minor], across(step)).start(),
        )
        mate_copy(core, source).start()

    repeat(major - 1, from_major)

    def relayed(number):
        home = near_first(number)
        source = (home // minor) * minor + (column + 1) % minor
        net_copy(source, minor_send.at[row], source).wait_recv()
        mate_copy(core, source).start()

    if minor > 1:
        repeat(major - 1, relayed)

    def from_mate(number):
        source = (me + 1 + number) % tok_count
        mate_copy(mate, source).wait_recv()

    repeat(tok_count - 1, from_mate)

    for number in (7, 8, 9):
        loads[number].wait()
    block = gathered.shape[2]
    group = math.gcd(tok_count, 8)
    groups = tok_count // group
    group_rows = group * block

    def project(number):
        def part_rows(part):
            return jnp.concatenate(
                [gathered[part, number * group + step].astype(f32) for step in range(group)],
                axis=0,
            ).astype(bf16)

        rows = jnp.concatenate([part_rows(0), part_rows(1)], axis=1)
        keys[number] = jnp.dot(rows, wk[...], preferred_element_type=f32).astype(bf16)
        values[number] = jnp.dot(rows, wv[...], preferred_element_type=f32).astype(bf16)

    repeat(groups, project)

    lane = lax.broadcasted_iota(jnp.int32, (cells, pair_width), 1)
    first = lane < head_dim
    inverse_root = 1.0 / math.sqrt(head_dim)
    ctx_copies = []
    for pair in range(pairs):
        span = slice(pair * pair_width, (pair + 1) * pair_width)
        pair_queries = queries[:, span].astype(f32)
        stacked = jnp.concatenate(
            [jnp.where(first, pair_queries, 0.0), jnp.where(first, 0.0, pair_queries)], axis=0
        ).astype(bf16)
        multiplier = jnp.concatenate(
            [
                jnp.broadcast_to(scale[0:1, 2 * pair + step : 2 * pair + step + 1], (cells, 1))
                for step in range(2)
            ],
            axis=0,
        ) * inverse_root

        def score(number):
            return (
                lax.dot_general(
                    stacked,
                    keys[number, :, span],
                    (((1,), (1,)), ((), ())),
                    preferred_element_type=f32,
                )
                * multiplier
            )

        def weigh(number, exp_scores):
            return jnp.dot(
                exp_scores.astype(bf16), values[number, :, span], preferred_element_type=f32
            )

        scores = score(0)
        row_max = jnp.max(scores, axis=1, keepdims=True)
        exp_scores = jnp.exp(scores - row_max)
        denominator = jnp.sum(exp_scores, axis=1, keepdims=True)
        total = weigh(0, exp_scores)
        if groups > 1:

            def absorb(number, state):
                row_max, denominator, total = state
                scores = score(number)
                new_max = jnp.maximum(row_max, jnp.max(scores, axis=1, keepdims=True))
                shrink = jnp.exp(row_max - new_max)
                exp_scores = jnp.exp(scores - new_max)
                denominator = denominator * shrink + jnp.sum(exp_scores, axis=1, keepdims=True)
                return new_max, denominator, total * shrink + weigh(number, exp_scores)

            row_max, denominator, total = lax.fori_loop(
                1, groups, absorb, (row_max, denominator, total)
            )
        total = total * (1.0 / denominator)
        context[0, pair] = jnp.where(first, total[:cells], total[cells:]).astype(bf16)
        ctx_copies.append(
            pltpu.make_async_remote_copy(
                src_ref=context.at[0, pair],
                dst_ref=context.at[1, pair],
                send_sem=ctx_send.at[pair],
                recv_sem=ctx_recv.at[pair],
                device_id={"head": mate},
            )
        )
        ctx_copies[-1].start()

    for number in (10, 11):
        loads[number].wait()

    def joined(which):
        return jnp.concatenate([context[which, pair] for pair in range(pairs)], axis=1)

    mine = joined(0)
    kept = jnp.dot(mine, wo[0, core], preferred_element_type=f32)
    rest = jnp.dot(mine, wo[0, mate], preferred_element_type=f32)
    for copy in wo_copies:
        copy.wait()
    for copy in ctx_copies:
        copy.wait()
    theirs = joined(1)
    kept = kept + jnp.dot(theirs, wo[1, core], preferred_element_type=f32)
    rest = rest + jnp.dot(theirs, wo[1, mate], preferred_element_type=f32)
    squares = jnp.sum(kept * kept, axis=1, keepdims=True) + jnp.sum(
        rest * rest, axis=1, keepdims=True
    )
    out_ref[...] = (kept * lax.rsqrt(squares / width + epsilon)).astype(bf16)

    repeat(
        major - 1,
        lambda number: net_copy(me, major_send.at[number], far_first(number)).wait_send(),
    )
    if minor > 1:
        repeat(
            major,
            lambda number: net_copy(me, minor_send.at[number], across(0)).wait_send(),
        )
    repeat(
        tok_count - 1,
        lambda number: mate_copy(core, (me + 1 + number) % tok_count).wait_send(),
    )


def solution(mesh):
    tok_count = mesh.shape["tok"]
    minor = 2 if tok_count % 2 == 0 and tok_count > 2 else 1

    def body(
        interior,
        boundary,
        vol_position,
        surf_position,
        vol_gain,
        surf_gain,
        wq,
        wk,
        wv,
        wo,
        scale,
    ):
        cells, width = interior.shape
        local_width = wq.shape[1]
        heads = scale.shape[0]
        pairs = heads // 2
        block = vol_position.shape[0] + surf_position.shape[0]
        group = math.gcd(tok_count, 8)
        groups = tok_count // group
        half = width // 2
        args = (
            interior,
            boundary,
            vol_position.reshape(1, -1),
            surf_position.reshape(1, -1),
            vol_gain.reshape(1, -1),
            surf_gain.reshape(1, -1),
            wq,
            wk,
            wv,
            wo,
            scale.reshape(1, -1),
        )
        held = [pltpu.VMEM(arg.shape, arg.dtype) for arg in args]
        held[9] = pltpu.VMEM((2, 2, local_width, half), bf16)
        dma = pltpu.SemaphoreType.DMA
        return pl.pallas_call(
            functools.partial(kernel, (tok_count, minor)),
            out_shape=jax.ShapeDtypeStruct((cells, width // mesh.shape["head"]), bf16),
            in_specs=[pl.BlockSpec(memory_space=pl.ANY)] * len(args),
            out_specs=pl.BlockSpec(memory_space=pltpu.VMEM),
            scratch_shapes=held
            + [
                pltpu.VMEM((2, tok_count, block, half), bf16),
                pltpu.VMEM((groups, group * block, local_width), bf16),
                pltpu.VMEM((groups, group * block, local_width), bf16),
                pltpu.VMEM((2, pairs, cells, local_width // pairs), bf16),
                dma((12,)),
                dma((tok_count // minor,)),
                dma((tok_count // minor,)),
                dma((tok_count,)),
                dma((tok_count,)),
                dma((tok_count,)),
                dma((2,)),
                dma((2,)),
                dma((pairs,)),
                dma((pairs,)),
            ],
            compiler_params=pltpu.CompilerParams(collective_id=0, has_side_effects=True),
        )(*args)

    placed = (
        P(("groups", "tok"), None),
        P(("groups", "tok"), None),
        P(("groups", "tok")),
        P(("groups", "tok")),
        P(),
        P(),
        P(None, "head"),
        P(None, "head"),
        P(None, "head"),
        P("head", None),
        P("head"),
    )
    return jax.shard_map(
        body, mesh=mesh, in_specs=placed, out_specs=P(("groups", "tok"), "head"), check_vma=False
    )
```

```python
import functools
import math

import jax
import jax.numpy as jnp
from jax import lax
from jax.experimental import pallas as pl
from jax.experimental.pallas import tpu as pltpu
from jax.sharding import PartitionSpec as P

epsilon = 1e-06
f32 = jnp.float32
bf16 = jnp.bfloat16


def repeat(count, step):
    if count <= 8:
        for number in range(count):
            step(number)
    else:
        pl.loop(0, count)(step)


def normed(values, gain):
    mean_square = jnp.mean(values * values, axis=1, keepdims=True)
    return (values * lax.rsqrt(mean_square + epsilon) * gain).astype(bf16)


def picked(positions, rows):
    lines = lax.broadcasted_iota(jnp.int32, (rows.shape[0], positions.shape[1]), 0)
    chosen = jnp.where(lines == positions, 1.0, 0.0).astype(bf16)
    return lax.dot_general(
        chosen, rows, (((0,), (0,)), ((), ())), preferred_element_type=f32
    )


def kernel(
    sizes,
    x_hbm,
    surf_hbm,
    vol_pos_hbm,
    surf_pos_hbm,
    vol_gain_hbm,
    surf_gain_hbm,
    wq_hbm,
    wk_hbm,
    wv_hbm,
    wo_hbm,
    scale_hbm,
    out_ref,
    x,
    surf,
    vol_pos,
    surf_pos,
    vol_gain,
    surf_gain,
    wq,
    wk,
    wv,
    wo,
    scale,
    gathered,
    keys,
    values,
    context,
    load_sem,
    major_send,
    minor_send,
    mate_send,
    net_recv,
    mate_recv,
    wo_send,
    wo_recv,
    ctx_send,
    ctx_recv,
):
    tok_count, minor = sizes
    major = tok_count // minor
    me = lax.axis_index("tok")
    core = lax.axis_index("head")
    mate = 1 - core
    row = me // minor
    column = me % minor
    width = x.shape[1]
    half = width // 2
    cells = x.shape[0]
    local_width = wq.shape[1]
    heads = scale.shape[1]
    head_dim = local_width // heads
    pair_width = 2 * head_dim
    pairs = heads // 2

    sources = (
        (x_hbm, x),
        (vol_pos_hbm, vol_pos),
        (surf_hbm, surf),
        (surf_pos_hbm, surf_pos),
        (vol_gain_hbm, vol_gain),
        (surf_gain_hbm, surf_gain),
        (wq_hbm, wq),
        (wk_hbm, wk),
        (wv_hbm, wv),
        (scale_hbm, scale),
    )
    loads = [
        pltpu.make_async_copy(source, target, load_sem.at[number])
        for number, (source, target) in enumerate(sources)
    ]
    for part in range(2):
        loads.append(
            pltpu.make_async_copy(
                wo_hbm.at[:, pl.ds(part * half, half)],
                wo.at[0, part],
                load_sem.at[len(sources) + part],
            )
        )
    for load in loads:
        load.start()

    side = (2 * row) // major

    def far_first(number):
        step = (major - 1 - number) * (1 - side) + (number + 1) * side
        return ((row + step) % major) * minor + column

    def near_first(number):
        step = (number + 1) * (1 - side) + (major - 1 - number) * side
        return ((row + step) % major) * minor + column

    def across(number):
        return row * minor + (column + 1 + number) % minor

    barrier = pltpu.get_barrier_semaphore()
    pl.semaphore_signal(barrier, inc=1, device_id={"head": mate})
    repeat(
        minor - 1,
        lambda number: pl.semaphore_signal(barrier, inc=1, device_id={"tok": across(number)}),
    )
    repeat(
        major - 1,
        lambda number: pl.semaphore_signal(barrier, inc=1, device_id={"tok": far_first(number)}),
    )

    for number in range(6):
        loads[number].wait()
    vol_anchor = normed(picked(vol_pos[...] - me * cells, x[...]), vol_gain[...])
    surf_anchor = normed(picked(surf_pos[...] - me * surf.shape[0], surf[...]), surf_gain[...])
    own = jnp.concatenate([vol_anchor.astype(f32), surf_anchor.astype(f32)], axis=0).astype(bf16)
    gathered[0, me] = own[:, :half]
    gathered[1, me] = own[:, half:]

    pl.semaphore_wait(barrier, major + minor - 1)

    def net_copy(source, send_sem, target):
        return pltpu.make_async_remote_copy(
            src_ref=gathered.at[core, source],
            dst_ref=gathered.at[core, source],
            send_sem=send_sem,
            recv_sem=net_recv.at[source],
            device_id={"tok": target},
        )

    def mate_copy(side_index, source):
        return pltpu.make_async_remote_copy(
            src_ref=gathered.at[side_index, source],
            dst_ref=gathered.at[side_index, source],
            send_sem=mate_send.at[source],
            recv_sem=mate_recv.at[source],
            device_id={"head": mate},
        )

    repeat(
        major - 1,
        lambda number: net_copy(me, major_send.at[number], far_first(number)).start(),
    )
    repeat(
        minor - 1,
        lambda number: net_copy(me, minor_send.at[row], across(number)).start(),
    )
    wo_copies = [
        pltpu.make_async_remote_copy(
            src_ref=wo_hbm.at[:, pl.ds(part * half, half)],
            dst_ref=wo.at[1, part],
            send_sem=wo_send.at[part],
            recv_sem=wo_recv.at[part],
            device_id={"head": mate},
        )
        for part in range(2)
    ]
    for copy in wo_copies:
        copy.start()

    cells_normed = normed(x[...].astype(f32), vol_gain[...])
    loads[6].wait()
    queries = jnp.dot(cells_normed, wq[...], preferred_element_type=f32).astype(bf16)

    def from_across(number):
        source = across(number)
        net_copy(source, minor_send.at[row], source).wait_recv()
        mate_copy(core, source).start()

    repeat(minor - 1, from_across)

    def from_major(number):
        source = near_first(number)
        net_copy(source, minor_send.at[row], source).wait_recv()
        repeat(
            minor - 1,
            lambda step: net_copy(source, minor_send.at[source // minor], across(step)).start(),
        )
        mate_copy(core, source).start()

    repeat(major - 1, from_major)

    def relayed(number):
        home = near_first(number)
        source = (home // minor) * minor + (column + 1) % minor
        net_copy(source, minor_send.at[row], source).wait_recv()
        mate_copy(core, source).start()

    if minor > 1:
        repeat(major - 1, relayed)

    def from_mate(number):
        source = (me + 1 + number) % tok_count
        mate_copy(mate, source).wait_recv()

    repeat(tok_count - 1, from_mate)

    for number in (7, 8, 9):
        loads[number].wait()
    block = gathered.shape[2]
    group = math.gcd(tok_count, 8)
    groups = tok_count // group
    group_rows = group * block

    def project(number):
        def part_rows(part):
            return jnp.concatenate(
                [gathered[part, number * group + step].astype(f32) for step in range(group)],
                axis=0,
            ).astype(bf16)

        rows = jnp.concatenate([part_rows(0), part_rows(1)], axis=1)
        keys[number] = jnp.dot(rows, wk[...], preferred_element_type=f32).astype(bf16)
        values[number] = jnp.dot(rows, wv[...], preferred_element_type=f32).astype(bf16)

    repeat(groups, project)

    lane = lax.broadcasted_iota(jnp.int32, (cells, pair_width), 1)
    first = lane < head_dim
    inverse_root = 1.0 / math.sqrt(head_dim)
    ctx_copies = []
    for pair in range(pairs):
        span = slice(pair * pair_width, (pair + 1) * pair_width)
        pair_queries = queries[:, span].astype(f32)
        stacked = jnp.concatenate(
            [jnp.where(first, pair_queries, 0.0), jnp.where(first, 0.0, pair_queries)], axis=0
        ).astype(bf16)
        multiplier = jnp.concatenate(
            [
                jnp.broadcast_to(scale[0:1, 2 * pair + step : 2 * pair + step + 1], (cells, 1))
                for step in range(2)
            ],
            axis=0,
        ) * inverse_root

        def score(number):
            return (
                lax.dot_general(
                    stacked,
                    keys[number, :, span],
                    (((1,), (1,)), ((), ())),
                    preferred_element_type=f32,
                )
                * multiplier
            )

        def weigh(number, exp_scores):
            return jnp.dot(
                exp_scores.astype(bf16), values[number, :, span], preferred_element_type=f32
            )

        scores = score(0)
        row_max = jnp.max(scores, axis=1, keepdims=True)
        exp_scores = jnp.exp(scores - row_max)
        denominator = jnp.sum(exp_scores, axis=1, keepdims=True)
        total = weigh(0, exp_scores)
        if groups > 1:

            def absorb(number, state):
                row_max, denominator, total = state
                scores = score(number)
                new_max = jnp.maximum(row_max, jnp.max(scores, axis=1, keepdims=True))
                shrink = jnp.exp(row_max - new_max)
                exp_scores = jnp.exp(scores - new_max)
                denominator = denominator * shrink + jnp.sum(exp_scores, axis=1, keepdims=True)
                return new_max, denominator, total * shrink + weigh(number, exp_scores)

            row_max, denominator, total = lax.fori_loop(
                1, groups, absorb, (row_max, denominator, total)
            )
        total = total * (1.0 / denominator)
        context[0, pair] = jnp.where(first, total[:cells], total[cells:]).astype(bf16)
        ctx_copies.append(
            pltpu.make_async_remote_copy(
                src_ref=context.at[0, pair],
                dst_ref=context.at[1, pair],
                send_sem=ctx_send.at[pair],
                recv_sem=ctx_recv.at[pair],
                device_id={"head": mate},
            )
        )
        ctx_copies[-1].start()

    for number in (10, 11):
        loads[number].wait()

    def joined(which):
        return jnp.concatenate([context[which, pair] for pair in range(pairs)], axis=1)

    mine = joined(0)
    kept = jnp.dot(mine, wo[0, core], preferred_element_type=f32)
    rest = jnp.dot(mine, wo[0, mate], preferred_element_type=f32)
    for copy in wo_copies:
        copy.wait()
    for copy in ctx_copies:
        copy.wait()
    theirs = joined(1)
    kept = kept + jnp.dot(theirs, wo[1, core], preferred_element_type=f32)
    rest = rest + jnp.dot(theirs, wo[1, mate], preferred_element_type=f32)
    squares = jnp.sum(kept * kept, axis=1, keepdims=True) + jnp.sum(
        rest * rest, axis=1, keepdims=True
    )
    out_ref[...] = (kept * lax.rsqrt(squares / width + epsilon)).astype(bf16)

    repeat(
        major - 1,
        lambda number: net_copy(me, major_send.at[number], far_first(number)).wait_send(),
    )
    if minor > 1:
        repeat(
            major,
            lambda number: net_copy(me, minor_send.at[number], across(0)).wait_send(),
        )
    repeat(
        tok_count - 1,
        lambda number: mate_copy(core, (me + 1 + number) % tok_count).wait_send(),
    )


def solution(mesh):
    tok_count = mesh.shape["tok"]
    minor = 1

    def body(
        interior,
        boundary,
        vol_position,
        surf_position,
        vol_gain,
        surf_gain,
        wq,
        wk,
        wv,
        wo,
        scale,
    ):
        cells, width = interior.shape
        local_width = wq.shape[1]
        heads = scale.shape[0]
        pairs = heads // 2
        block = vol_position.shape[0] + surf_position.shape[0]
        group = math.gcd(tok_count, 8)
        groups = tok_count // group
        half = width // 2
        args = (
            interior,
            boundary,
            vol_position.reshape(1, -1),
            surf_position.reshape(1, -1),
            vol_gain.reshape(1, -1),
            surf_gain.reshape(1, -1),
            wq,
            wk,
            wv,
            wo,
            scale.reshape(1, -1),
        )
        held = [pltpu.VMEM(arg.shape, arg.dtype) for arg in args]
        held[9] = pltpu.VMEM((2, 2, local_width, half), bf16)
        dma = pltpu.SemaphoreType.DMA
        return pl.pallas_call(
            functools.partial(kernel, (tok_count, minor)),
            out_shape=pltpu.VMEM((cells, width // mesh.shape["head"]), bf16),
            in_specs=[pl.BlockSpec(memory_space=pl.ANY)] * len(args),
            out_specs=pl.BlockSpec(memory_space=pltpu.VMEM),
            scratch_shapes=held
            + [
                pltpu.VMEM((2, tok_count, block, half), bf16),
                pltpu.VMEM((groups, group * block, local_width), bf16),
                pltpu.VMEM((groups, group * block, local_width), bf16),
                pltpu.VMEM((2, pairs, cells, local_width // pairs), bf16),
                dma((12,)),
                dma((tok_count // minor,)),
                dma((tok_count // minor,)),
                dma((tok_count,)),
                dma((tok_count,)),
                dma((tok_count,)),
                dma((2,)),
                dma((2,)),
                dma((pairs,)),
                dma((pairs,)),
            ],
            compiler_params=pltpu.CompilerParams(collective_id=0, has_side_effects=True),
        )(*args)

    placed = (
        P(("groups", "tok"), None),
        P(("groups", "tok"), None),
        P(("groups", "tok")),
        P(("groups", "tok")),
        P(),
        P(),
        P(None, "head"),
        P(None, "head"),
        P(None, "head"),
        P("head", None),
        P("head"),
    )
    return jax.shard_map(
        body, mesh=mesh, in_specs=placed, out_specs=P(("groups", "tok"), "head"), check_vma=False
    )
```

```python
import functools
import math

import jax
import jax.numpy as jnp
from jax import lax
from jax.experimental import pallas as pl
from jax.experimental.pallas import tpu as pltpu
from jax.sharding import PartitionSpec as P

epsilon = 1e-06
f32 = jnp.float32
bf16 = jnp.bfloat16
GROUP = 8


def repeat(count, step):
    if count <= 8:
        for number in range(count):
            step(number)
    else:
        pl.loop(0, count)(step)


def normed(values, gain):
    mean_square = jnp.mean(values * values, axis=1, keepdims=True)
    return (values * lax.rsqrt(mean_square + epsilon) * gain).astype(bf16)


def picked(positions, rows):
    lines = lax.broadcasted_iota(jnp.int32, (rows.shape[0], positions.shape[1]), 0)
    chosen = jnp.where(lines == positions, 1.0, 0.0).astype(bf16)
    return lax.dot_general(
        chosen, rows, (((0,), (0,)), ((), ())), preferred_element_type=f32
    )


def kernel(
    sizes,
    x_hbm,
    surf_hbm,
    vol_pos_hbm,
    surf_pos_hbm,
    vol_gain_hbm,
    surf_gain_hbm,
    wq_hbm,
    wk_hbm,
    wv_hbm,
    wo_hbm,
    scale_hbm,
    out_ref,
    x,
    surf,
    vol_pos,
    surf_pos,
    vol_gain,
    surf_gain,
    wq,
    wk,
    wv,
    wo,
    scale,
    gathered,
    run_max,
    run_sum,
    run_total,
    context,
    load_sem,
    net_send,
    mate_send,
    net_recv,
    mate_recv,
    wo_send,
    wo_recv,
    ctx_send,
    ctx_recv,
):
    tok_count, minor = sizes
    major = tok_count // minor
    me = lax.axis_index("tok")
    core = lax.axis_index("head")
    mate = 1 - core
    row = me // minor
    column = me % minor
    width = x.shape[1]
    half = width // 2
    cells = x.shape[0]
    local_width = wq.shape[1]
    heads = scale.shape[1]
    head_dim = local_width // heads
    pair_width = 2 * head_dim
    pairs = heads // 2

    sources = (
        (x_hbm, x),
        (vol_pos_hbm, vol_pos),
        (surf_hbm, surf),
        (surf_pos_hbm, surf_pos),
        (vol_gain_hbm, vol_gain),
        (surf_gain_hbm, surf_gain),
        (wq_hbm, wq),
        (wk_hbm, wk),
        (wv_hbm, wv),
        (scale_hbm, scale),
    )
    loads = [
        pltpu.make_async_copy(source, target, load_sem.at[number])
        for number, (source, target) in enumerate(sources)
    ]
    for part in range(2):
        loads.append(
            pltpu.make_async_copy(
                wo_hbm.at[:, pl.ds(part * half, half)],
                wo.at[0, part],
                load_sem.at[len(sources) + part],
            )
        )
    for load in loads:
        load.start()

    side = (2 * row) // major

    def source_of(number):
        step = number // minor
        step = step * (1 - side) + (major - step) * side
        return ((row + step) % major) * minor + (column + number) % minor

    def far_first(number):
        return source_of(tok_count - 1 - number)

    def near_first(number):
        return source_of(number + 1)

    peers = tok_count - 1
    barrier = pltpu.get_barrier_semaphore()
    repeat(
        peers,
        lambda number: pl.semaphore_signal(barrier, inc=1, device_id={"tok": far_first(number)}),
    )
    pl.semaphore_signal(barrier, inc=1, device_id={"head": mate})

    for number in range(6):
        loads[number].wait()
    vol_anchor = normed(picked(vol_pos[...] - me * cells, x[...]), vol_gain[...])
    surf_anchor = normed(picked(surf_pos[...] - me * surf.shape[0], surf[...]), surf_gain[...])
    own = jnp.concatenate([vol_anchor.astype(f32), surf_anchor.astype(f32)], axis=0).astype(bf16)
    gathered[0, me] = own[:, :half]
    gathered[1, me] = own[:, half:]

    pl.semaphore_wait(barrier, peers + 1)

    def net_copy(number, source, target):
        return pltpu.make_async_remote_copy(
            src_ref=gathered.at[core, source],
            dst_ref=gathered.at[core, source],
            send_sem=net_send.at[number],
            recv_sem=net_recv.at[source],
            device_id={"tok": target},
        )

    def mate_copy(side_index, source):
        return pltpu.make_async_remote_copy(
            src_ref=gathered.at[side_index, source],
            dst_ref=gathered.at[side_index, source],
            send_sem=mate_send.at[source],
            recv_sem=mate_recv.at[source],
            device_id={"head": mate},
        )

    repeat(peers, lambda number: net_copy(number, me, far_first(number)).start())
    wo_copies = [
        pltpu.make_async_remote_copy(
            src_ref=wo_hbm.at[:, pl.ds(part * half, half)],
            dst_ref=wo.at[1, part],
            send_sem=wo_send.at[part],
            recv_sem=wo_recv.at[part],
            device_id={"head": mate},
        )
        for part in range(2)
    ]
    for copy in wo_copies:
        copy.start()

    cells_normed = normed(x[...].astype(f32), vol_gain[...])
    loads[6].wait()
    queries = jnp.dot(cells_normed, wq[...], preferred_element_type=f32).astype(bf16)

    def from_net(number):
        source = near_first(number)
        net_copy(0, source, source).wait_recv()
        mate_copy(core, source).start()

    repeat(peers, from_net)

    for number in (7, 8, 9):
        loads[number].wait()

    lane = lax.broadcasted_iota(jnp.int32, (cells, pair_width), 1)
    first = lane < head_dim
    inverse_root = 1.0 / math.sqrt(head_dim)
    stacked = []
    multipliers = []
    for pair in range(pairs):
        pair_queries = queries[:, pair * pair_width : (pair + 1) * pair_width].astype(f32)
        stacked.append(
            jnp.concatenate(
                [jnp.where(first, pair_queries, 0.0), jnp.where(first, 0.0, pair_queries)],
                axis=0,
            ).astype(bf16)
        )
        multipliers.append(
            jnp.concatenate(
                [
                    jnp.broadcast_to(
                        scale[0:1, 2 * pair + step : 2 * pair + step + 1], (cells, 1)
                    )
                    for step in range(2)
                ],
                axis=0,
            )
            * inverse_root
        )

    group = math.gcd(tok_count, GROUP)
    groups = tok_count // group

    def joined_rows(number):
        parts = [
            jnp.concatenate(
                [
                    gathered[part, source_of(number * group + step)].astype(f32)
                    for step in range(group)
                ],
                axis=0,
            ).astype(bf16)
            for part in range(2)
        ]
        return jnp.concatenate(parts, axis=1)

    def fold(number, finish):
        rows = joined_rows(number)
        keys = jnp.dot(rows, wk[...], preferred_element_type=f32).astype(bf16)
        values = jnp.dot(rows, wv[...], preferred_element_type=f32).astype(bf16)
        started = not (isinstance(number, int) and number == 0)
        for pair in range(pairs):
            span = slice(pair * pair_width, (pair + 1) * pair_width)
            scores = (
                lax.dot_general(
                    stacked[pair],
                    keys[:, span],
                    (((1,), (1,)), ((), ())),
                    preferred_element_type=f32,
                )
                * multipliers[pair]
            )
            row_max = jnp.max(scores, axis=1, keepdims=True)
            if started:
                row_max = jnp.maximum(row_max, run_max[pair])
            exp_scores = jnp.exp(scores - row_max)
            denominator = jnp.sum(exp_scores, axis=1, keepdims=True)
            total = jnp.dot(
                exp_scores.astype(bf16), values[:, span], preferred_element_type=f32
            )
            if started:
                shrink = jnp.exp(run_max[pair] - row_max)
                denominator = denominator + run_sum[pair] * shrink
                total = total + run_total[pair] * shrink
            if finish is None:
                run_max[pair] = row_max
                run_sum[pair] = denominator
                run_total[pair] = total
            else:
                finish(pair, total * (1.0 / denominator))

    def from_mate(number):
        mate_copy(mate, source_of(number)).wait_recv()

    ctx_copies = [
        pltpu.make_async_remote_copy(
            src_ref=context.at[0, pair],
            dst_ref=context.at[1, pair],
            send_sem=ctx_send.at[pair],
            recv_sem=ctx_recv.at[pair],
            device_id={"head": mate},
        )
        for pair in range(pairs)
    ]

    def finish(pair, total):
        context[0, pair] = jnp.where(first, total[:cells], total[cells:]).astype(bf16)
        ctx_copies[pair].start()

    repeat(group - 1, lambda number: from_mate(number + 1))
    if groups > 1:
        fold(0, None)
    if groups > 2:

        def middle(number):
            repeat(group, lambda step: from_mate((number + 1) * group + step))
            fold(number + 1, None)

        pl.loop(0, groups - 2)(middle)
    if groups > 1:
        repeat(group, lambda number: from_mate((groups - 1) * group + number))
    fold(groups - 1, finish)

    for number in (10, 11):
        loads[number].wait()

    def joined(which):
        return jnp.concatenate([context[which, pair] for pair in range(pairs)], axis=1)

    mine = joined(0)
    kept = jnp.dot(mine, wo[0, core], preferred_element_type=f32)
    rest = jnp.dot(mine, wo[0, mate], preferred_element_type=f32)
    for copy in wo_copies:
        copy.wait()
    span = local_width // 2
    for part in range(2):
        chosen = range(part * pairs // 2, (part + 1) * pairs // 2)
        for pair in chosen:
            ctx_copies[pair].wait()
        theirs = jnp.concatenate([context[1, pair] for pair in chosen], axis=1)
        rows = slice(part * span, (part + 1) * span)
        kept = kept + jnp.dot(theirs, wo[1, core, rows], preferred_element_type=f32)
        rest = rest + jnp.dot(theirs, wo[1, mate, rows], preferred_element_type=f32)
    squares = jnp.sum(kept * kept, axis=1, keepdims=True) + jnp.sum(
        rest * rest, axis=1, keepdims=True
    )
    out_ref[...] = (kept * lax.rsqrt(squares / width + epsilon)).astype(bf16)

    def drain(number):
        net_copy(number, me, far_first(number)).wait_send()
        mate_copy(core, near_first(number)).wait_send()

    repeat(peers, drain)


def solution(mesh):
    tok_count = mesh.shape["tok"]
    minor = 2 if tok_count % 2 == 0 else 1

    def body(
        interior,
        boundary,
        vol_position,
        surf_position,
        vol_gain,
        surf_gain,
        wq,
        wk,
        wv,
        wo,
        scale,
    ):
        cells, width = interior.shape
        local_width = wq.shape[1]
        heads = scale.shape[0]
        pairs = heads // 2
        block = vol_position.shape[0] + surf_position.shape[0]
        half = width // 2
        args = (
            interior,
            boundary,
            vol_position.reshape(1, -1),
            surf_position.reshape(1, -1),
            vol_gain.reshape(1, -1),
            surf_gain.reshape(1, -1),
            wq,
            wk,
            wv,
            wo,
            scale.reshape(1, -1),
        )
        held = [pltpu.VMEM(arg.shape, arg.dtype) for arg in args]
        held[9] = pltpu.VMEM((2, 2, local_width, half), bf16)
        dma = pltpu.SemaphoreType.DMA
        return pl.pallas_call(
            functools.partial(kernel, (tok_count, minor)),
            out_shape=pltpu.VMEM((cells, width // mesh.shape["head"]), bf16),
            in_specs=[pl.BlockSpec(memory_space=pl.ANY)] * len(args),
            out_specs=pl.BlockSpec(memory_space=pltpu.VMEM),
            scratch_shapes=held
            + [
                pltpu.VMEM((2, tok_count, block, half), bf16),
                pltpu.VMEM((pairs, 2 * cells, 1), f32),
                pltpu.VMEM((pairs, 2 * cells, 1), f32),
                pltpu.VMEM((pairs, 2 * cells, local_width // pairs), f32),
                pltpu.VMEM((2, pairs, cells, local_width // pairs), bf16),
                dma((12,)),
                dma((tok_count,)),
                dma((tok_count,)),
                dma((tok_count,)),
                dma((tok_count,)),
                dma((2,)),
                dma((2,)),
                dma((pairs,)),
                dma((pairs,)),
            ],
            compiler_params=pltpu.CompilerParams(collective_id=0, has_side_effects=True),
        )(*args)

    placed = (
        P(("groups", "tok"), None),
        P(("groups", "tok"), None),
        P(("groups", "tok")),
        P(("groups", "tok")),
        P(),
        P(),
        P(None, "head"),
        P(None, "head"),
        P(None, "head"),
        P("head", None),
        P("head"),
    )
    return jax.shard_map(
        body, mesh=mesh, in_specs=placed, out_specs=P(("groups", "tok"), "head"), check_vma=False
    )
```
